128 devices in a mesh: fsdp: 64 (over z, y, x), tensor: 2 (over core).
Axes of the slice: x: 4, y: 4, z: 4, core: 2. Of those that a mesh axis runs over, the one named last changes fastest.
Arguments:
- weights: bfloat16 [64, 1792, 256], P(None, 'fsdp', 'tensor'), may hold values from -0.125 to 0.125
- gradient: bfloat16 [64, 1792, 256], P(None, 'fsdp', 'tensor'), may hold values from -6 to 6
- moment_first: float32 [64, 1792, 256], P('fsdp', None, 'tensor'), may hold values from -4 to 4
- moment_second: float32 [64, 1792, 256], P('fsdp', None, 'tensor'), may hold values from 0.05 to 4
- statistics: float32 [64, 8, 256, 256], P('fsdp', 'tensor'), may hold values from -0.4 to 4.4, as said below
- eigenbases: float32 [64, 8, 256, 256], P('fsdp', 'tensor'), may hold values from -0.2 to 1.2
Outputs:
- new_weights: bfloat16 [64, 1792, 256], P(None, 'fsdp', 'tensor')
- new_first: float32 [64, 1792, 256], P('fsdp', None, 'tensor')
- new_second: float32 [64, 1792, 256], P('fsdp', None, 'tensor')
- new_statistics: float32 [64, 8, 256, 256], P('fsdp', 'tensor')
- new_bases: float32 [64, 8, 256, 256], P('fsdp', 'tensor')
The draws below stay inside these ranges and needn't reach their ends.
Inputs may be any that keep to these rules, and one draw needn't show every extreme that they name: `statistics`: symmetric matrices.
All inputs are finite; a program needn't handle non-finite values.
Results may differ from the reference program's by a relative error of at most 0.0095.
Values may be sent and summed in bfloat16 or wider, within the bound.
A program may use at most 64 MiB of HBM per device.

```python
import math
import jax
import jax.numpy as jnp
from jax import lax

D = 1792
FD = 256
BLOCK = 256
NS_STEPS = 5
STEP = 10
NBLK = 7
FACT = 8
NMAT = 64


def draw_statistics(key, part):
    key_noise, key_diag = jax.random.split(key)
    noise_field = jnp.clip(jax.random.normal(key_noise, (NMAT, FACT, BLOCK, BLOCK), jnp.float32), -4.0, 4.0)
    symmetric = (noise_field + jnp.swapaxes(noise_field, 2, 3)) * 0.05
    diagonal = jax.random.uniform(key_diag, (NMAT, FACT, BLOCK), jnp.float32, 1.0, 4.0)
    identity = jnp.eye(BLOCK, dtype=jnp.float32)
    return symmetric * (1.0 - identity) + diagonal[..., None] * identity


def draw_eigenbases(key, part):
    noise_field = jax.random.normal(key, (NMAT, FACT, BLOCK, BLOCK), jnp.float32)
    scaled = jnp.clip(noise_field * (0.6 / math.sqrt(BLOCK)), -0.15, 0.15)
    identity = jnp.eye(BLOCK, dtype=jnp.float32)
    return identity + scaled * (1.0 - identity)


def block_scale(key, extent, cuts, least, top_value):
    level = 1.0
    for dim, parts in cuts:
        draws = jax.random.uniform(jax.random.fold_in(jax.random.fold_in(key, 6), dim), (parts,), jnp.float32, least / len(cuts), top_value / len(cuts))
        level = level * jnp.repeat(jnp.exp(draws), extent[dim] // parts).reshape((-1,) + (1,) * (len(extent) - 1 - dim))
    return level


def centred(own_key, dims, width, limit, cuts=(), kind=jnp.bfloat16):
    result = width * jax.random.normal(own_key, dims, jnp.float32)
    if cuts:
        result = result * block_scale(own_key, dims, cuts, -0.22, 0.18)
    return jnp.clip(result, -limit, limit).astype(kind)


def setup_inputs(seed: int = 0) -> dict:
    keys = jax.random.split(jax.random.key(seed), 7)
    weights = centred(keys[0], (NMAT, D, FD), D ** -0.5, 0.125, ((1, 64), (2, 2)))
    gradient = centred(keys[1], (NMAT, D, FD), 1.0, 6.0, ((1, 64), (2, 2)))
    moment_first = centred(keys[2], (NMAT, D, FD), 0.5, 4.0, ((0, 64), (2, 2)), jnp.float32)
    moment_second = jnp.clip(jnp.exp(math.log(4.0) - 4.3820266 * jax.random.uniform(keys[3], (NMAT, D, FD), jnp.float32) ** block_scale(keys[3], (NMAT, D, FD), ((0, 64), (2, 2)), -0.2, 0.2)), 0.05, 4.0)
    statistics = draw_statistics(jax.random.fold_in(keys[6], 71), 0)
    eigenbases = draw_eigenbases(jax.random.fold_in(keys[6], 71), 0)
    return dict(weights=weights, gradient=gradient, moment_first=moment_first, moment_second=moment_second, statistics=statistics, eigenbases=eigenbases)


HIGH = lax.Precision.HIGHEST

def orthogonal(stat_block, basis):
    grown = jnp.dot(stat_block, basis, precision=HIGH)
    ortho = grown / (jnp.sqrt(jnp.sum(grown * grown)) + 1e-06)
    for sweep in range(NS_STEPS):
        inner = jnp.dot(ortho.T, ortho, precision=HIGH)
        ortho = 1.5 * ortho - 0.5 * jnp.dot(ortho, inner, precision=HIGH)
    return ortho

def one_matrix(packed):
    weight_mat, grad_mat, first_mat, second_mat, stat_mat, basis_mat = packed
    basis_low = basis_mat.astype(jnp.bfloat16)
    right_low = basis_low[NBLK]
    left_low = basis_low[:NBLK]
    half_turn = jnp.dot(grad_mat, right_low, preferred_element_type=jnp.float32).astype(jnp.bfloat16)
    rotated = jnp.einsum('kij,kil->kjl', left_low.astype(jnp.float32), half_turn.reshape(NBLK, BLOCK, FD).astype(jnp.float32)).reshape(D, FD)
    first_new = 0.9 * first_mat + 0.1 * rotated
    second_new = 0.95 * second_mat + 0.05 * rotated * rotated
    direction = (first_new / (1.0 - 0.9 ** STEP) / (jnp.sqrt(second_new / (1.0 - 0.95 ** STEP)) + 1e-08)).astype(jnp.bfloat16)
    turned_back = jnp.dot(direction, right_low.T, preferred_element_type=jnp.float32).astype(jnp.bfloat16)
    update = jnp.einsum('kij,kjl->kil', left_low.astype(jnp.float32), turned_back.reshape(NBLK, BLOCK, FD).astype(jnp.float32)).reshape(D, FD).astype(jnp.bfloat16)
    weight_full = weight_mat.astype(jnp.float32)
    weight_new = (weight_full - 0.01 * (update.astype(jnp.float32) + 0.1 * weight_full)).astype(jnp.bfloat16)
    grad_blocks = grad_mat.reshape(NBLK, BLOCK, FD).astype(jnp.float32)
    left_gram = jnp.einsum('kij,klj->kil', grad_blocks, grad_blocks)
    right_gram = jnp.dot(grad_mat.T, grad_mat, preferred_element_type=jnp.float32)
    gram = jnp.concatenate([left_gram, right_gram[None]], axis=0)
    stat_new = 0.95 * stat_mat + 0.05 * gram
    basis_new = jax.vmap(orthogonal)(stat_new, basis_mat)
    return (weight_new, first_new, second_new, stat_new, basis_new)

def reference(weights, gradient, moment_first, moment_second, statistics, eigenbases):
    results = lax.map(one_matrix, (weights, gradient, moment_first, moment_second, statistics, eigenbases))
    return (results[0], results[1], results[2], results[3], results[4])
```

```python
import jax
import jax.numpy as jnp
from jax import lax
from jax.sharding import PartitionSpec as P

NS_STEPS = 5
STEP = 10


HIGH = lax.Precision.HIGH
SWAP = ((0, 1), (1, 0))


def both(column_index, mine, axis):
    other = lax.ppermute(mine, "tensor", SWAP)
    first = jnp.where(column_index == 0, mine, other)
    second = jnp.where(column_index == 0, other, mine)
    return jnp.concatenate([first, second], axis=axis)


def orthogonal(stat_block, basis):
    grown = jnp.dot(stat_block, basis, precision=HIGH)
    ortho = grown / (jnp.sqrt(jnp.sum(grown * grown)) + 1e-06)
    for sweep in range(NS_STEPS):
        inner = jnp.dot(ortho.T, ortho, precision=HIGH)
        ortho = 1.5 * ortho - 0.5 * jnp.dot(ortho, inner, precision=HIGH)
    return ortho


def body(weights, gradient, moment_first, moment_second, statistics, eigenbases):
    column_index = lax.axis_index("tensor")
    block = eigenbases.shape[2]
    local_cols = gradient.shape[2]
    whole_rows = moment_first.shape[1]
    num_blocks = whole_rows // block
    per_device = eigenbases.shape[1]
    owned = lax.all_to_all(gradient, "fsdp", split_axis=0, concat_axis=1, tiled=True)
    grad_full = both(column_index, owned[0], 1)
    bases_all = both(column_index, eigenbases[0].astype(jnp.bfloat16), 0)
    right_low = bases_all[num_blocks]
    left_low = bases_all[:num_blocks]
    col_start = column_index * local_cols
    right_cols = lax.dynamic_slice_in_dim(right_low, col_start, local_cols, 1)
    half_turn = jnp.dot(grad_full, right_cols, preferred_element_type=jnp.float32).astype(
        jnp.bfloat16
    )
    rotated = jnp.einsum(
        "kij,kil->kjl",
        left_low,
        half_turn.reshape(num_blocks, block, local_cols),
        preferred_element_type=jnp.float32,
    ).reshape(whole_rows, local_cols)
    first_new = 0.9 * moment_first[0] + 0.1 * rotated
    second_new = 0.95 * moment_second[0] + 0.05 * rotated * rotated
    direction = (
        first_new / (1.0 - 0.9**STEP) / (jnp.sqrt(second_new / (1.0 - 0.95**STEP)) + 1e-08)
    ).astype(jnp.bfloat16)
    right_rows = lax.dynamic_slice_in_dim(right_low, col_start, local_cols, 0)
    turned_back = lax.dot_general(
        both(column_index, direction, 1),
        right_rows,
        (((1,), (1,)), ((), ())),
        preferred_element_type=jnp.float32,
    ).astype(jnp.bfloat16)
    update = (
        jnp.einsum(
            "kij,kjl->kil",
            left_low,
            turned_back.reshape(num_blocks, block, local_cols),
            preferred_element_type=jnp.float32,
        )
        .reshape(whole_rows, local_cols)
        .astype(jnp.bfloat16)
    )
    update_rows = lax.all_to_all(
        update[None], "fsdp", split_axis=1, concat_axis=0, tiled=True
    ).astype(jnp.float32)
    weight_full = weights.astype(jnp.float32)
    weight_new = (weight_full - 0.01 * (update_rows + 0.1 * weight_full)).astype(jnp.bfloat16)

    def left_gram(index):
        rows_block = lax.dynamic_slice_in_dim(grad_full, index * block, block, 0)
        return lax.dot_general(
            rows_block, rows_block, (((1,), (1,)), ((), ())), preferred_element_type=jnp.float32
        )

    def right_gram(index):
        return lax.dot_general(
            grad_full, grad_full, (((0,), (0,)), ((), ())), preferred_element_type=jnp.float32
        )

    stat_list = []
    basis_list = []
    for member in range(per_device):
        factor_index = column_index * per_device + member
        gram = lax.cond(factor_index < num_blocks, left_gram, right_gram, factor_index)
        stat_new = 0.95 * statistics[0, member] + 0.05 * gram
        stat_list.append(stat_new)
        basis_list.append(orthogonal(stat_new, eigenbases[0, member]))
    stat_out = jnp.stack(stat_list)[None]
    basis_out = jnp.stack(basis_list)[None]
    return (weight_new, first_new[None], second_new[None], stat_out, basis_out)


def solution(mesh):
    placed = (
        P(None, "fsdp", "tensor"),
        P(None, "fsdp", "tensor"),
        P("fsdp", None, "tensor"),
        P("fsdp", None, "tensor"),
        P("fsdp", "tensor", None, None),
        P("fsdp", "tensor", None, None),
    )
    return jax.shard_map(
        body,
        mesh=mesh,
        in_specs=placed,
        out_specs=(
            P(None, "fsdp", "tensor"),
            P("fsdp", None, "tensor"),
            P("fsdp", None, "tensor"),
            P("fsdp", "tensor", None, None),
            P("fsdp", "tensor", None, None),
        ),
        check_vma=False,
    )
```

```python
import functools

import jax
import jax.numpy as jnp
from jax import lax
from jax.experimental import pallas as pl
from jax.experimental.pallas import tpu as pltpu
from jax.sharding import PartitionSpec as P

NS_STEPS = 5
STEP = 10
MESH = pl.DeviceIdType.MESH
LOW = jnp.bfloat16
NN = (((1,), (0,)), ((), ()))
NT = (((1,), (1,)), ((), ()))
TN = (((0,), (0,)), ((), ()))


def product(a, b, dims):
    return lax.dot_general(a, b, dims, preferred_element_type=jnp.float32)


def halves(x):
    high = x.astype(LOW)
    return high, (x - high.astype(jnp.float32)).astype(LOW)


def product3(a, b, dims):
    return (
        product(a[0], b[1], dims) + product(a[1], b[0], dims) + product(a[0], b[0], dims)
    )


def kernel(
    ndev,
    weights, gradient, moment_first, moment_second, statistics, eigenbases,
    new_weights, new_first, new_second, new_statistics, new_bases,
    grad_mine, grad_other, grad_wide, grad_full, bases_low, dir_mine, dir_other,
    update_wide, update_out, update_in,
    send_grad, recv_grad, send_update, recv_update,
    send_pair, recv_pair, send_dir, recv_dir, local_sem,
):
    me = lax.axis_index("fsdp")
    core = lax.axis_index("tensor")
    other = 1 - core
    part = gradient.shape[1]
    cols = gradient.shape[2]
    per = eigenbases.shape[0]
    block = eigenbases.shape[1]
    rows = moment_first.shape[0]
    nblk = rows // block
    my_cols = pl.ds(pl.multiple_of(core * cols, cols), cols)
    other_cols = pl.ds(pl.multiple_of(other * cols, cols), cols)

    for j in range(per):
        bases_low[core * per + j] = eigenbases[j].astype(LOW)

    barrier = pltpu.get_barrier_semaphore()

    def greet(i, carry):
        pl.semaphore_signal(
            barrier, inc=1, device_id=(lax.rem(me + i, ndev), core), device_id_type=MESH
        )
        return carry

    lax.fori_loop(1, ndev, greet, 0)
    pl.semaphore_signal(barrier, inc=1, device_id=(me, other), device_id_type=MESH)
    pl.semaphore_wait(barrier, ndev)

    def grad_copy(i):
        peer = lax.rem(me + i, ndev)
        return pltpu.make_async_remote_copy(
            src_ref=gradient.at[peer],
            dst_ref=grad_mine.at[me],
            send_sem=send_grad.at[i],
            recv_sem=recv_grad.at[i],
            device_id=(peer, core),
            device_id_type=MESH,
        )

    def update_copy(i):
        peer = lax.rem(me + i, ndev)
        return pltpu.make_async_remote_copy(
            src_ref=update_out.at[peer],
            dst_ref=update_in.at[me],
            send_sem=send_update.at[i],
            recv_sem=recv_update.at[i],
            device_id=(peer, core),
            device_id_type=MESH,
        )

    def grad_wait(i):
        source = lax.rem(me + ndev - i, ndev)
        return pltpu.make_async_remote_copy(
            src_ref=gradient.at[source],
            dst_ref=grad_mine.at[source],
            send_sem=send_grad.at[i],
            recv_sem=recv_grad.at[i],
            device_id=(source, core),
            device_id_type=MESH,
        )

    def update_wait(i):
        source = lax.rem(me + ndev - i, ndev)
        return pltpu.make_async_remote_copy(
            src_ref=update_out.at[source],
            dst_ref=update_in.at[source],
            send_sem=send_update.at[i],
            recv_sem=recv_update.at[i],
            device_id=(source, core),
            device_id_type=MESH,
        )

    def start(make):
        def step(i, carry):
            make(i).start()
            return carry

        lax.fori_loop(1, ndev, step, 0)

    def arrived(make):
        def step(i, carry):
            make(i).wait_recv()
            return carry

        lax.fori_loop(1, ndev, step, 0)

    def sent(make):
        def step(i, carry):
            make(i).wait_send()
            return carry

        lax.fori_loop(1, ndev, step, 0)

    start(grad_copy)
    own = pltpu.make_async_copy(gradient.at[me], grad_mine.at[me], local_sem.at[0])
    own.start()
    mine = bases_low.at[pl.ds(core * per, per)]
    share_bases = pltpu.make_async_remote_copy(
        src_ref=mine,
        dst_ref=mine,
        send_sem=send_pair.at[0],
        recv_sem=recv_pair.at[0],
        device_id=(me, other),
        device_id_type=MESH,
    )
    share_bases.start()
    own.wait()
    arrived(grad_wait)
    share_grad = pltpu.make_async_remote_copy(
        src_ref=grad_mine,
        dst_ref=grad_other,
        send_sem=send_pair.at[1],
        recv_sem=recv_pair.at[1],
        device_id=(me, other),
        device_id_type=MESH,
    )
    share_grad.start()

    for s in range(ndev):
        grad_wide[s * part : (s + 1) * part, :] = grad_mine[s].astype(jnp.float32)
    grad_full[:, my_cols] = grad_wide[...].astype(LOW)
    share_bases.wait()
    share_grad.wait()
    for s in range(ndev):
        grad_wide[s * part : (s + 1) * part, :] = grad_other[s].astype(jnp.float32)
    grad_full[:, other_cols] = grad_wide[...].astype(LOW)

    right_cols = bases_low[nblk, :, my_cols]

    def dir_copy(k):
        here = pl.ds(k * block, block)
        return pltpu.make_async_remote_copy(
            src_ref=dir_mine.at[here],
            dst_ref=dir_other.at[here],
            send_sem=send_dir.at[k],
            recv_sem=recv_dir.at[k],
            device_id=(me, other),
            device_id_type=MESH,
        )

    for k in range(nblk):
        here = slice(k * block, (k + 1) * block)
        half_turn = product(grad_full[here, :], right_cols, NN).astype(LOW)
        rotated = product(bases_low[k], half_turn, TN)
        first = 0.9 * moment_first[here, :] + 0.1 * rotated
        second = 0.95 * moment_second[here, :] + 0.05 * rotated * rotated
        new_first[here, :] = first
        new_second[here, :] = second
        dir_mine[here, :] = (
            first / (1.0 - 0.9**STEP) / (jnp.sqrt(second / (1.0 - 0.95**STEP)) + 1e-08)
        ).astype(LOW)
        if k >= 1:
            dir_copy(k - 1).start()

    def put_gram(j, gram):
        new_statistics[j] = 0.95 * statistics[j] + 0.05 * gram

    def left_gram(j):
        g = grad_full[pl.ds(pl.multiple_of((core * per + j) * block, block), block), :]
        put_gram(j, product(g, g, NT))

    left_gram(0)
    dir_copy(nblk - 1).start()
    for j in range(1, per - 1):
        left_gram(j)

    @pl.when(core == 0)
    def _():
        left_gram(per - 1)

    @pl.when(core == 1)
    def _():
        put_gram(per - 1, product(grad_full[...], grad_full[...], TN))

    right_rows = bases_low.at[nblk]
    rows_mine = right_rows[my_cols, my_cols]
    rows_other = right_rows[my_cols, other_cols]
    for k in range(nblk):
        here = slice(k * block, (k + 1) * block)
        dir_copy(k).wait()
        turned = product(dir_mine[here, :], rows_mine, NT)
        turned = (turned + product(dir_other[here, :], rows_other, NT)).astype(LOW)
        update = product(bases_low[k], turned, NN).astype(LOW)
        update_wide[here, :] = update.astype(jnp.float32)
    for s in range(ndev):
        update_out[s] = update_wide[s * part : (s + 1) * part, :].astype(LOW)

    growns = []
    for j in range(per):
        grown = product3(halves(new_statistics[j]), halves(eigenbases[j]), NN)
        growns.append(grown)
        new_bases[j] = grown / (jnp.sqrt(jnp.sum(grown * grown)) + 1e-06)

    start(update_copy)
    own = pltpu.make_async_copy(update_out.at[me], update_in.at[me], local_sem.at[1])
    own.start()

    def sweep(step, carry):
        for j in range(per):
            x = new_bases[j]
            parts = halves(x)
            outer = product3(parts, parts, NT)
            new_bases[j] = 1.5 * x - 0.5 * product3(halves(outer), parts, NN)
        return carry

    lax.fori_loop(0, NS_STEPS, sweep, 0)
    sent(grad_copy)
    own.wait()
    arrived(update_wait)

    def finish(s, carry):
        w = weights[s].astype(jnp.float32)
        u = update_in[s].astype(jnp.float32)
        new_weights[s] = (w - 0.01 * (u + 0.1 * w)).astype(LOW)
        return carry

    lax.fori_loop(0, ndev, finish, 0)
    sent(update_copy)


def body(ndev, weights, gradient, moment_first, moment_second, statistics, eigenbases):
    part, cols = gradient.shape[1:]
    rows = moment_first.shape[1]
    per, block = eigenbases.shape[1:3]
    nblk = rows // block
    vmem = pl.BlockSpec(memory_space=pltpu.VMEM)
    f32 = jnp.float32
    dma = pltpu.SemaphoreType.DMA
    inputs = (
        weights, gradient, moment_first[0], moment_second[0], statistics[0], eigenbases[0]
    )
    outs = pl.pallas_call(
        functools.partial(kernel, ndev),
        out_shape=(
            jax.ShapeDtypeStruct(weights.shape, LOW),
            jax.ShapeDtypeStruct((rows, cols), f32),
            jax.ShapeDtypeStruct((rows, cols), f32),
            jax.ShapeDtypeStruct((per, block, block), f32),
            jax.ShapeDtypeStruct((per, block, block), f32),
        ),
        in_specs=[vmem] * 6,
        out_specs=[vmem] * 5,
        scratch_shapes=[
            pltpu.VMEM((ndev, part, cols), LOW),
            pltpu.VMEM((ndev, part, cols), LOW),
            pltpu.VMEM((rows, cols), f32),
            pltpu.VMEM((rows, 2 * cols), LOW),
            pltpu.VMEM((2 * per, block, block), LOW),
            pltpu.VMEM((rows, cols), LOW),
            pltpu.VMEM((rows, cols), LOW),
            pltpu.VMEM((rows, cols), f32),
            pltpu.VMEM((ndev, part, cols), LOW),
            pltpu.VMEM((ndev, part, cols), LOW),
            dma((ndev,)),
            dma((ndev,)),
            dma((ndev,)),
            dma((ndev,)),
            dma((2,)),
            dma((2,)),
            dma((nblk,)),
            dma((nblk,)),
            dma((2,)),
        ],
        compiler_params=pltpu.CompilerParams(
            collective_id=0, has_side_effects=True, vmem_limit_bytes=48 * 1024 * 1024
        ),
    )(*inputs)
    return (outs[0],) + tuple(o[None] for o in outs[1:])


def solution(mesh):
    placed = (
        P(None, "fsdp", "tensor"),
        P(None, "fsdp", "tensor"),
        P("fsdp", None, "tensor"),
        P("fsdp", None, "tensor"),
        P("fsdp", "tensor", None, None),
        P("fsdp", "tensor", None, None),
    )
    return jax.shard_map(
        functools.partial(body, mesh.shape["fsdp"]),
        mesh=mesh,
        in_specs=placed,
        out_specs=(placed[0],) + placed[2:],
        check_vma=False,
    )
```

```python
import functools

import jax
import jax.numpy as jnp
from jax import lax
from jax.experimental import pallas as pl
from jax.experimental.pallas import tpu as pltpu
from jax.sharding import PartitionSpec as P

NS_STEPS = 5
STEP = 10
MESH = pl.DeviceIdType.MESH
LOW = jnp.bfloat16
NN = (((1,), (0,)), ((), ()))
NT = (((1,), (1,)), ((), ()))
TN = (((0,), (0,)), ((), ()))


def product(a, b, dims):
    return lax.dot_general(a, b, dims, preferred_element_type=jnp.float32)


def halves(x):
    high = x.astype(LOW)
    return high, (x - high.astype(jnp.float32)).astype(LOW)


def product3(a, b, dims):
    return (
        product(a[0], b[1], dims) + product(a[1], b[0], dims) + product(a[0], b[0], dims)
    )


def kernel(
    ndev,
    weights, gradient, moment_first, moment_second, statistics, eigenbases,
    new_weights, new_first, new_second, new_statistics, new_bases,
    grad_mine, grad_other, grad_wide, grad_full, bases_low, dir_mine, dir_other,
    update_wide, update_out, update_in,
    send_grad, recv_grad, send_update, recv_update,
    send_pair, recv_pair, send_share, recv_share, send_dir, recv_dir, local_sem,
):
    me = lax.axis_index("fsdp")
    core = lax.axis_index("tensor")
    other = 1 - core
    part = gradient.shape[1]
    cols = gradient.shape[2]
    per = eigenbases.shape[0]
    block = eigenbases.shape[1]
    rows = moment_first.shape[0]
    nblk = rows // block
    my_cols = pl.ds(pl.multiple_of(core * cols, cols), cols)
    other_cols = pl.ds(pl.multiple_of(other * cols, cols), cols)

    for j in range(per):
        bases_low[core * per + j] = eigenbases[j].astype(LOW)

    barrier = pltpu.get_barrier_semaphore()

    def greet(i, carry):
        pl.semaphore_signal(
            barrier, inc=1, device_id=(lax.rem(me + i, ndev), core), device_id_type=MESH
        )
        return carry

    lax.fori_loop(1, ndev, greet, 0)
    pl.semaphore_signal(barrier, inc=1, device_id=(me, other), device_id_type=MESH)
    pl.semaphore_wait(barrier, ndev)

    def grad_copy(i):
        peer = lax.rem(me + i, ndev)
        return pltpu.make_async_remote_copy(
            src_ref=gradient.at[peer],
            dst_ref=grad_mine.at[me],
            send_sem=send_grad.at[i],
            recv_sem=recv_grad.at[i],
            device_id=(peer, core),
            device_id_type=MESH,
        )

    def update_copy(i):
        peer = lax.rem(me + i, ndev)
        return pltpu.make_async_remote_copy(
            src_ref=update_out.at[peer],
            dst_ref=update_in.at[me],
            send_sem=send_update.at[i],
            recv_sem=recv_update.at[i],
            device_id=(peer, core),
            device_id_type=MESH,
        )

    def grad_wait(i):
        source = lax.rem(me + ndev - i, ndev)
        return pltpu.make_async_remote_copy(
            src_ref=gradient.at[source],
            dst_ref=grad_mine.at[source],
            send_sem=send_grad.at[i],
            recv_sem=recv_grad.at[i],
            device_id=(source, core),
            device_id_type=MESH,
        )

    def update_wait(i):
        source = lax.rem(me + ndev - i, ndev)
        return pltpu.make_async_remote_copy(
            src_ref=update_out.at[source],
            dst_ref=update_in.at[source],
            send_sem=send_update.at[i],
            recv_sem=recv_update.at[i],
            device_id=(source, core),
            device_id_type=MESH,
        )

    def start(make):
        def step(i, carry):
            make(i).start()
            return carry

        lax.fori_loop(1, ndev, step, 0)

    def arrived(make):
        def step(i, carry):
            make(i).wait_recv()
            return carry

        lax.fori_loop(1, ndev, step, 0)

    def sent(make):
        def step(i, carry):
            make(i).wait_send()
            return carry

        lax.fori_loop(1, ndev, step, 0)

    start(grad_copy)
    own = pltpu.make_async_copy(gradient.at[me], grad_mine.at[me], local_sem.at[0])
    own.start()
    mine = bases_low.at[pl.ds(core * per, per)]
    share_bases = pltpu.make_async_remote_copy(
        src_ref=mine,
        dst_ref=mine,
        send_sem=send_pair.at[0],
        recv_sem=recv_pair.at[0],
        device_id=(me, other),
        device_id_type=MESH,
    )
    share_bases.start()

    def share(i):
        source = lax.rem(me + ndev - i, ndev)
        return pltpu.make_async_remote_copy(
            src_ref=grad_mine.at[source],
            dst_ref=grad_other.at[source],
            send_sem=send_share.at[i],
            recv_sem=recv_share.at[i],
            device_id=(me, other),
            device_id_type=MESH,
        )

    own.wait()
    share(0).start()

    def forward(i, carry):
        grad_wait(i).wait_recv()
        share(i).start()
        return carry

    lax.fori_loop(1, ndev, forward, 0)

    for s in range(ndev):
        grad_wide[s * part : (s + 1) * part, :] = grad_mine[s].astype(jnp.float32)
    grad_full[:, my_cols] = grad_wide[...].astype(LOW)
    share_bases.wait()
    share(0).wait_recv()
    arrived(share)
    for s in range(ndev):
        grad_wide[s * part : (s + 1) * part, :] = grad_other[s].astype(jnp.float32)
    grad_full[:, other_cols] = grad_wide[...].astype(LOW)

    right_cols = bases_low[nblk, :, my_cols]

    def dir_copy(k):
        here = pl.ds(k * block, block)
        return pltpu.make_async_remote_copy(
            src_ref=dir_mine.at[here],
            dst_ref=dir_other.at[here],
            send_sem=send_dir.at[k],
            recv_sem=recv_dir.at[k],
            device_id=(me, other),
            device_id_type=MESH,
        )

    for k in range(nblk):
        here = slice(k * block, (k + 1) * block)
        half_turn = product(grad_full[here, :], right_cols, NN).astype(LOW)
        rotated = product(bases_low[k], half_turn, TN)
        first = 0.9 * moment_first[here, :] + 0.1 * rotated
        second = 0.95 * moment_second[here, :] + 0.05 * rotated * rotated
        new_first[here, :] = first
        new_second[here, :] = second
        dir_mine[here, :] = (
            first / (1.0 - 0.9**STEP) / (jnp.sqrt(second / (1.0 - 0.95**STEP)) + 1e-08)
        ).astype(LOW)
        if k >= 1:
            dir_copy(k - 1).start()

    def put_gram(j, gram):
        new_statistics[j] = 0.95 * statistics[j] + 0.05 * gram

    def left_gram(j):
        g = grad_full[pl.ds(pl.multiple_of((core * per + j) * block, block), block), :]
        put_gram(j, product(g, g, NT))

    left_gram(0)
    dir_copy(nblk - 1).start()

    right_rows = bases_low.at[nblk]
    rows_mine = right_rows[my_cols, my_cols]
    rows_other = right_rows[my_cols, other_cols]
    for k in range(nblk):
        here = slice(k * block, (k + 1) * block)
        dir_copy(k).wait()
        turned = product(dir_mine[here, :], rows_mine, NT)
        turned = (turned + product(dir_other[here, :], rows_other, NT)).astype(LOW)
        update = product(bases_low[k], turned, NN).astype(LOW)
        update_wide[here, :] = update.astype(jnp.float32)
    for s in range(ndev):
        update_out[s] = update_wide[s * part : (s + 1) * part, :].astype(LOW)

    left_gram(1)
    start(update_copy)
    own = pltpu.make_async_copy(update_out.at[me], update_in.at[me], local_sem.at[1])
    own.start()

    for j in range(2, per - 1):
        left_gram(j)

    @pl.when(core == 0)
    def _():
        left_gram(per - 1)

    @pl.when(core == 1)
    def _():
        put_gram(per - 1, product(grad_full[...], grad_full[...], TN))

    for j in range(per):
        grown = product3(halves(new_statistics[j]), halves(eigenbases[j]), NN)
        new_bases[j] = grown / (jnp.sqrt(jnp.sum(grown * grown)) + 1e-06)

    def sweep(step, carry):
        for j in range(per):
            x = new_bases[j]
            parts = halves(x)
            outer = product3(parts, parts, NT)
            new_bases[j] = 1.5 * x - 0.5 * product3(halves(outer), parts, NN)
        return carry

    lax.fori_loop(0, NS_STEPS, sweep, 0)
    sent(grad_copy)
    share(0).wait_send()
    sent(share)
    own.wait()
    arrived(update_wait)

    def finish(s, carry):
        w = weights[s].astype(jnp.float32)
        u = update_in[s].astype(jnp.float32)
        new_weights[s] = (w - 0.01 * (u + 0.1 * w)).astype(LOW)
        return carry

    lax.fori_loop(0, ndev, finish, 0)
    sent(update_copy)


def body(ndev, weights, gradient, moment_first, moment_second, statistics, eigenbases):
    part, cols = gradient.shape[1:]
    rows = moment_first.shape[1]
    per, block = eigenbases.shape[1:3]
    nblk = rows // block
    vmem = pl.BlockSpec(memory_space=pltpu.VMEM)
    f32 = jnp.float32
    dma = pltpu.SemaphoreType.DMA
    inputs = (
        weights, gradient, moment_first[0], moment_second[0], statistics[0], eigenbases[0]
    )
    outs = pl.pallas_call(
        functools.partial(kernel, ndev),
        out_shape=(
            jax.ShapeDtypeStruct(weights.shape, LOW),
            jax.ShapeDtypeStruct((rows, cols), f32),
            jax.ShapeDtypeStruct((rows, cols), f32),
            jax.ShapeDtypeStruct((per, block, block), f32),
            jax.ShapeDtypeStruct((per, block, block), f32),
        ),
        in_specs=[vmem] * 6,
        out_specs=[vmem] * 5,
        scratch_shapes=[
            pltpu.VMEM((ndev, part, cols), LOW),
            pltpu.VMEM((ndev, part, cols), LOW),
            pltpu.VMEM((rows, cols), f32),
            pltpu.VMEM((rows, 2 * cols), LOW),
            pltpu.VMEM((2 * per, block, block), LOW),
            pltpu.VMEM((rows, cols), LOW),
            pltpu.VMEM((rows, cols), LOW),
            pltpu.VMEM((rows, cols), f32),
            pltpu.VMEM((ndev, part, cols), LOW),
            pltpu.VMEM((ndev, part, cols), LOW),
            dma((ndev,)),
            dma((ndev,)),
            dma((ndev,)),
            dma((ndev,)),
            dma((1,)),
            dma((1,)),
            dma((ndev,)),
            dma((ndev,)),
            dma((nblk,)),
            dma((nblk,)),
            dma((2,)),
        ],
        compiler_params=pltpu.CompilerParams(
            collective_id=0, has_side_effects=True, vmem_limit_bytes=24 * 1024 * 1024
        ),
    )(*inputs)
    return (outs[0],) + tuple(o[None] for o in outs[1:])


def solution(mesh):
    placed = (
        P(None, "fsdp", "tensor"),
        P(None, "fsdp", "tensor"),
        P("fsdp", None, "tensor"),
        P("fsdp", None, "tensor"),
        P("fsdp", "tensor", None, None),
        P("fsdp", "tensor", None, None),
    )
    return jax.shard_map(
        functools.partial(body, mesh.shape["fsdp"]),
        mesh=mesh,
        in_specs=placed,
        out_specs=(placed[0],) + placed[2:],
        check_vma=False,
    )
```

```python
import functools

import jax
import jax.numpy as jnp
from jax import lax
from jax.experimental import pallas as pl
from jax.experimental.pallas import tpu as pltpu
from jax.sharding import PartitionSpec as P

NS_STEPS = 5
STEP = 10
MESH = pl.DeviceIdType.MESH
LOW = jnp.bfloat16
NN = (((1,), (0,)), ((), ()))
NT = (((1,), (1,)), ((), ()))
TN = (((0,), (0,)), ((), ()))


def product(a, b, dims):
    return lax.dot_general(a, b, dims, preferred_element_type=jnp.float32)


def halves(x):
    high = x.astype(LOW)
    return high, (x - high.astype(jnp.float32)).astype(LOW)


def product3(a, b, dims):
    return (
        product(a[0], b[1], dims) + product(a[1], b[0], dims) + product(a[0], b[0], dims)
    )


def kernel(
    ndev,
    weights, gradient, first_hbm, second_hbm, statistics_hbm, eigenbases_hbm,
    new_weights, new_first, new_second, new_statistics, new_bases,
    grad_mine, grad_other, grad_wide, grad_full, bases_low, dir_mine, dir_other,
    update_wide, update_out, update_in,
    moment_first, moment_second, statistics, eigenbases,
    send_grad, recv_grad, send_update, recv_update,
    send_pair, recv_pair, send_share, recv_share, send_dir, recv_dir, local_sem,
):
    me = lax.axis_index("fsdp")
    core = lax.axis_index("tensor")
    other = 1 - core
    part = gradient.shape[1]
    cols = gradient.shape[2]
    per = eigenbases.shape[0]
    block = eigenbases.shape[1]
    rows = moment_first.shape[0]
    nblk = rows // block
    my_cols = pl.ds(pl.multiple_of(core * cols, cols), cols)
    other_cols = pl.ds(pl.multiple_of(other * cols, cols), cols)

    loads = [
        pltpu.make_async_copy(src, dst, local_sem.at[2 + n])
        for n, (src, dst) in enumerate(
            (
                (eigenbases_hbm, eigenbases),
                (first_hbm, moment_first),
                (second_hbm, moment_second),
                (statistics_hbm, statistics),
            )
        )
    ]
    for load in loads:
        load.start()

    barrier = pltpu.get_barrier_semaphore()

    def greet(i, carry):
        pl.semaphore_signal(
            barrier, inc=1, device_id=(lax.rem(me + i, ndev), core), device_id_type=MESH
        )
        return carry

    lax.fori_loop(1, ndev, greet, 0)
    pl.semaphore_signal(barrier, inc=1, device_id=(me, other), device_id_type=MESH)
    loads[0].wait()
    for j in range(per):
        bases_low[core * per + j] = eigenbases[j].astype(LOW)
    pl.semaphore_wait(barrier, ndev)

    def grad_copy(i):
        peer = lax.rem(me + i, ndev)
        return pltpu.make_async_remote_copy(
            src_ref=gradient.at[peer],
            dst_ref=grad_mine.at[me],
            send_sem=send_grad.at[i],
            recv_sem=recv_grad.at[i],
            device_id=(peer, core),
            device_id_type=MESH,
        )

    def update_copy(i):
        peer = lax.rem(me + i, ndev)
        return pltpu.make_async_remote_copy(
            src_ref=update_out.at[peer],
            dst_ref=update_in.at[me],
            send_sem=send_update.at[i],
            recv_sem=recv_update.at[i],
            device_id=(peer, core),
            device_id_type=MESH,
        )

    def grad_wait(i):
        source = lax.rem(me + ndev - i, ndev)
        return pltpu.make_async_remote_copy(
            src_ref=gradient.at[source],
            dst_ref=grad_mine.at[source],
            send_sem=send_grad.at[i],
            recv_sem=recv_grad.at[i],
            device_id=(source, core),
            device_id_type=MESH,
        )

    def update_wait(i):
        source = lax.rem(me + ndev - i, ndev)
        return pltpu.make_async_remote_copy(
            src_ref=update_out.at[source],
            dst_ref=update_in.at[source],
            send_sem=send_update.at[i],
            recv_sem=recv_update.at[i],
            device_id=(source, core),
            device_id_type=MESH,
        )

    def start(make):
        def step(i, carry):
            make(i).start()
            return carry

        lax.fori_loop(1, ndev, step, 0)

    def arrived(make):
        def step(i, carry):
            make(i).wait_recv()
            return carry

        lax.fori_loop(1, ndev, step, 0)

    def sent(make):
        def step(i, carry):
            make(i).wait_send()
            return carry

        lax.fori_loop(1, ndev, step, 0)

    start(grad_copy)
    own = pltpu.make_async_copy(gradient.at[me], grad_mine.at[me], local_sem.at[0])
    own.start()
    mine = bases_low.at[pl.ds(core * per, per)]
    share_bases = pltpu.make_async_remote_copy(
        src_ref=mine,
        dst_ref=mine,
        send_sem=send_pair.at[0],
        recv_sem=recv_pair.at[0],
        device_id=(me, other),
        device_id_type=MESH,
    )
    share_bases.start()

    def share(i):
        source = lax.rem(me + ndev - i, ndev)
        return pltpu.make_async_remote_copy(
            src_ref=grad_mine.at[source],
            dst_ref=grad_other.at[source],
            send_sem=send_share.at[i],
            recv_sem=recv_share.at[i],
            device_id=(me, other),
            device_id_type=MESH,
        )

    own.wait()
    share(0).start()

    def forward(i, carry):
        grad_wait(i).wait_recv()
        share(i).start()
        return carry

    lax.fori_loop(1, ndev, forward, 0)
    for load in loads[1:]:
        load.wait()

    for s in range(ndev):
        grad_wide[s * part : (s + 1) * part, :] = grad_mine[s].astype(jnp.float32)
    grad_full[:, my_cols] = grad_wide[...].astype(LOW)
    share_bases.wait()
    share(0).wait_recv()
    arrived(share)
    for s in range(ndev):
        grad_wide[s * part : (s + 1) * part, :] = grad_other[s].astype(jnp.float32)
    grad_full[:, other_cols] = grad_wide[...].astype(LOW)

    right_cols = bases_low[nblk, :, my_cols]

    def dir_copy(k):
        here = pl.ds(k * block, block)
        return pltpu.make_async_remote_copy(
            src_ref=dir_mine.at[here],
            dst_ref=dir_other.at[here],
            send_sem=send_dir.at[k],
            recv_sem=recv_dir.at[k],
            device_id=(me, other),
            device_id_type=MESH,
        )

    for k in range(nblk):
        here = slice(k * block, (k + 1) * block)
        half_turn = product(grad_full[here, :], right_cols, NN).astype(LOW)
        rotated = product(bases_low[k], half_turn, TN)
        first = 0.9 * moment_first[here, :] + 0.1 * rotated
        second = 0.95 * moment_second[here, :] + 0.05 * rotated * rotated
        new_first[here, :] = first
        new_second[here, :] = second
        dir_mine[here, :] = (
            first / (1.0 - 0.9**STEP) / (jnp.sqrt(second / (1.0 - 0.95**STEP)) + 1e-08)
        ).astype(LOW)
        if k >= 1:
            dir_copy(k - 1).start()

    def put_gram(j, gram):
        new_statistics[j] = 0.95 * statistics[j] + 0.05 * gram

    def left_gram(j):
        g = grad_full[pl.ds(pl.multiple_of((core * per + j) * block, block), block), :]
        put_gram(j, product(g, g, NT))

    left_gram(0)
    dir_copy(nblk - 1).start()

    right_rows = bases_low.at[nblk]
    rows_mine = right_rows[my_cols, my_cols]
    rows_other = right_rows[my_cols, other_cols]
    for k in range(nblk):
        here = slice(k * block, (k + 1) * block)
        dir_copy(k).wait()
        turned = product(dir_mine[here, :], rows_mine, NT)
        turned = (turned + product(dir_other[here, :], rows_other, NT)).astype(LOW)
        update = product(bases_low[k], turned, NN).astype(LOW)
        update_wide[here, :] = update.astype(jnp.float32)
    for s in range(ndev):
        update_out[s] = update_wide[s * part : (s + 1) * part, :].astype(LOW)

    left_gram(1)
    start(update_copy)
    own = pltpu.make_async_copy(update_out.at[me], update_in.at[me], local_sem.at[1])
    own.start()

    for j in range(2, per - 1):
        left_gram(j)

    @pl.when(core == 0)
    def _():
        left_gram(per - 1)

    @pl.when(core == 1)
    def _():
        put_gram(per - 1, product(grad_full[...], grad_full[...], TN))

    for j in range(per):
        grown = product3(halves(new_statistics[j]), halves(eigenbases[j]), NN)
        new_bases[j] = grown / (jnp.sqrt(jnp.sum(grown * grown)) + 1e-06)

    def sweep(step, carry):
        for j in range(per):
            x = new_bases[j]
            parts = halves(x)
            outer = product3(parts, parts, NT)
            new_bases[j] = 1.5 * x - 0.5 * product3(halves(outer), parts, NN)
        return carry

    lax.fori_loop(0, NS_STEPS, sweep, 0)
    sent(grad_copy)
    share(0).wait_send()
    sent(share)
    own.wait()
    arrived(update_wait)

    def finish(s, carry):
        w = weights[s].astype(jnp.float32)
        u = update_in[s].astype(jnp.float32)
        new_weights[s] = (w - 0.01 * (u + 0.1 * w)).astype(LOW)
        return carry

    lax.fori_loop(0, ndev, finish, 0)
    sent(update_copy)


def body(ndev, weights, gradient, moment_first, moment_second, statistics, eigenbases):
    part, cols = gradient.shape[1:]
    rows = moment_first.shape[1]
    per, block = eigenbases.shape[1:3]
    nblk = rows // block
    vmem = pl.BlockSpec(memory_space=pltpu.VMEM)
    f32 = jnp.float32
    dma = pltpu.SemaphoreType.DMA
    inputs = (
        weights, gradient, moment_first[0], moment_second[0], statistics[0], eigenbases[0]
    )
    inputs = inputs[:2] + tuple(
        pltpu.with_memory_space_constraint(x, pltpu.HBM) for x in inputs[2:]
    )
    outs = pl.pallas_call(
        functools.partial(kernel, ndev),
        out_shape=(
            jax.ShapeDtypeStruct(weights.shape, LOW),
            jax.ShapeDtypeStruct((rows, cols), f32),
            jax.ShapeDtypeStruct((rows, cols), f32),
            jax.ShapeDtypeStruct((per, block, block), f32),
            jax.ShapeDtypeStruct((per, block, block), f32),
        ),
        in_specs=[vmem] * 2 + [pl.BlockSpec(memory_space=pltpu.HBM)] * 4,
        out_specs=[vmem] * 5,
        scratch_shapes=[
            pltpu.VMEM((ndev, part, cols), LOW),
            pltpu.VMEM((ndev, part, cols), LOW),
            pltpu.VMEM((rows, cols), f32),
            pltpu.VMEM((rows, 2 * cols), LOW),
            pltpu.VMEM((2 * per, block, block), LOW),
            pltpu.VMEM((rows, cols), LOW),
            pltpu.VMEM((rows, cols), LOW),
            pltpu.VMEM((rows, cols), f32),
            pltpu.VMEM((ndev, part, cols), LOW),
            pltpu.VMEM((ndev, part, cols), LOW),
            pltpu.VMEM((rows, cols), f32),
            pltpu.VMEM((rows, cols), f32),
            pltpu.VMEM((per, block, block), f32),
            pltpu.VMEM((per, block, block), f32),
            dma((ndev,)),
            dma((ndev,)),
            dma((ndev,)),
            dma((ndev,)),
            dma((1,)),
            dma((1,)),
            dma((ndev,)),
            dma((ndev,)),
            dma((nblk,)),
            dma((nblk,)),
            dma((6,)),
        ],
        compiler_params=pltpu.CompilerParams(
            collective_id=0, has_side_effects=True, vmem_limit_bytes=24 * 1024 * 1024
        ),
    )(*inputs)
    return (outs[0],) + tuple(o[None] for o in outs[1:])


def solution(mesh):
    placed = (
        P(None, "fsdp", "tensor"),
        P(None, "fsdp", "tensor"),
        P("fsdp", None, "tensor"),
        P("fsdp", None, "tensor"),
        P("fsdp", "tensor", None, None),
        P("fsdp", "tensor", None, None),
    )
    return jax.shard_map(
        functools.partial(body, mesh.shape["fsdp"]),
        mesh=mesh,
        in_specs=placed,
        out_specs=(placed[0],) + placed[2:],
        check_vma=False,
    )
```
